128 devices in a mesh: dp: 32 (over x, z_hi, y), tensor: 4 (over z_lo, core).
Axes of the slice: x: 4, y: 4, z: 4 (z_hi: 2, z_lo: 2; z = z_hi * 2 + z_lo), core: 2. Of those that a mesh axis runs over, the one named last changes fastest.
Arguments:
- activations: bfloat16 [8192, 8192], P('dp'), may hold values from -6 to 6
- out_grad: bfloat16 [8192, 2048], P('dp', 'tensor'), may hold values from -6 to 6
- weight: bfloat16 [8192, 2048], P(None, 'tensor'), may hold values from -0.0625 to 0.0625
- left_stats: float32 [8192, 2048], P('dp', 'tensor'), may hold values from -100 to 100, as said below
- right_stats: float32 [8192, 2048], P('dp', 'tensor'), may hold values from -100 to 100, as said below
Outputs:
- input_grad: bfloat16 [8192, 8192], P('dp', 'tensor')
- update: bfloat16 [8192, 2048], P('dp', 'tensor')
- left_new: float32 [8192, 2048], P('dp', 'tensor')
- right_new: float32 [8192, 2048], P('dp', 'tensor')
The draws below stay inside these ranges and needn't reach their ends.
Inputs may be any that keep to these rules, and one draw needn't show every extreme that they name: `left_stats`: every 512 x 512 block at rows i * 512 and columns j * 512 is symmetric and positive definite. `right_stats`: every 512 x 512 block at rows i * 512 and columns j * 512 is symmetric and positive definite.
All inputs are finite; a program needn't handle non-finite values.
Results may differ from the reference program's by a relative error of at most 0.001.
Values may be sent and summed in bfloat16 or wider, within the bound.
No kernel may reach another device: no remote copies, remote signals or barrier semaphores. Data moves between devices by JAX's collectives and lax.ppermute only.
A program may use at most 128 MiB of HBM per device.

```python
import math
import jax
import jax.numpy as jnp
from jax import lax

D = 8192
F = 2048
BLOCK = 512
ITERS = 10
TOKENS = 8192


def draw_statistic(key):
    block_total = D // BLOCK * (F // BLOCK)
    first_key, second_key = jax.random.split(key, 2)
    factors = jax.random.truncated_normal(first_key, -3.0, 3.0, (block_total, BLOCK, BLOCK), jnp.float32)
    products = jnp.einsum('bik,bjk->bij', factors, factors) / BLOCK
    diagonal = jnp.exp(jax.random.uniform(second_key, (block_total, BLOCK), jnp.float32, math.log(0.1), 0.0))
    products = products + diagonal[:, :, None] * jnp.eye(BLOCK, dtype=jnp.float32)
    shaped = products.reshape(D // BLOCK, F // BLOCK, BLOCK, BLOCK)
    return shaped.transpose(0, 2, 1, 3).reshape(D, F)


def draw_left_stats(key, part):
    return draw_statistic(jax.random.fold_in(key, 11))


def draw_right_stats(key, part):
    return draw_statistic(jax.random.fold_in(key, 23))


def with_spikes(values, rng, source, target, parts, factor):
    def block_of(dim):
        return (jnp.arange(values.shape[dim]) // (values.shape[dim] // parts)).reshape((-1,) + (1,) * (values.ndim - 1 - dim))

    one_side = jax.random.permutation(rng, parts)[block_of(target)]
    second = (block_of(target) + parts // 2) % parts
    return jnp.where((block_of(source) == one_side) | (block_of(source) == second), factor * values, values)


def steps_of(stream_key, shape, pieces, low, top_value):
    loudness, own = 1.0, jax.random.fold_in(stream_key, 6)
    for dim, parts in pieces:
        steps = jnp.exp(jax.random.uniform(jax.random.fold_in(own, dim), (parts,), jnp.float32, low / len(pieces), top_value / len(pieces)))
        loudness = loudness * jnp.repeat(steps, shape[dim] // parts).reshape([-1 if axis == dim else 1 for axis in range(len(shape))])
    return loudness


def normal_values(key, extent, width, bound, cuts=(), held_as=jnp.bfloat16):
    factor_of = steps_of(key, extent, cuts, -0.22, 0.18) if cuts else 1.0
    values = jax.random.normal(key, extent, jnp.float32) * width * factor_of
    return jnp.minimum(jnp.maximum(values, -bound), bound).astype(held_as)


def heavy_noise(rng, shape, width, most, pieces, heavy, kind=jnp.bfloat16):
    array = width * jax.random.normal(rng, shape, jnp.float32)
    if pieces:
        array = array * steps_of(rng, shape, pieces, -0.22, 0.18)
    return jnp.clip(with_spikes(array, jax.random.fold_in(rng, 3), *heavy), -most, most).astype(kind)


def setup_inputs(seed: int = 0) -> dict:
    keys = jax.random.split(jax.random.key(seed), 6)
    activations = heavy_noise(keys[0], (TOKENS, D), 1.0, 6.0, ((0, 32),), (0, 1, 32, 2.75))
    out_grad = normal_values(keys[1], (TOKENS, F), 1.0, 6.0, ((0, 32), (1, 4)))
    weight = normal_values(keys[2], (D, F), D ** -0.5, 0.0625, ((1, 4),))
    left_stats = draw_left_stats(jax.random.fold_in(keys[5], 71), 0)
    right_stats = draw_right_stats(jax.random.fold_in(keys[5], 71), 0)
    return {"activations": activations, "out_grad": out_grad, "weight": weight, "left_stats": left_stats, "right_stats": right_stats}


decay_rate = 0.9

def batch_product(form, first, second):
    return jnp.einsum(form, first, second, precision=lax.Precision.HIGHEST)

def inverse_root(matrix):
    identity = jnp.eye(matrix.shape[-1], dtype=matrix.dtype)
    frobenius = jnp.sqrt(lax.optimization_barrier(jnp.sum(matrix * matrix, axis=(1, 2), keepdims=True)))
    current = matrix / frobenius
    result = jnp.broadcast_to(identity, matrix.shape)
    for iteration in range(ITERS):
        factor = (5.0 * identity - current) / 4.0
        result = batch_product('bij,bjk->bik', result, factor)
        squared = batch_product('bij,bjk->bik', factor, factor)
        fourth = batch_product('bij,bjk->bik', squared, squared)
        current = batch_product('bij,bjk->bik', fourth, current)
    return result / jnp.sqrt(jnp.sqrt(frobenius))

def split_blocks(whole_rows):
    row_total, col_total = whole_rows.shape
    shaped = whole_rows.reshape(row_total // BLOCK, BLOCK, col_total // BLOCK, BLOCK)
    return shaped.transpose(0, 2, 1, 3).reshape(-1, BLOCK, BLOCK)

def join_blocks(blocks, row_total, col_total):
    shaped = blocks.reshape(row_total // BLOCK, col_total // BLOCK, BLOCK, BLOCK)
    return shaped.transpose(0, 2, 1, 3).reshape(row_total, col_total)

def reference(activations, out_grad, weight, left_stats, right_stats):
    weight_grad = jnp.dot(activations.T, out_grad, preferred_element_type=jnp.float32) * TOKENS ** (-0.5)
    input_grad = jnp.dot(out_grad, weight.T, preferred_element_type=jnp.float32).astype(jnp.bfloat16)
    grad_blocks = split_blocks(weight_grad)
    left_gram = decay_rate * split_blocks(left_stats) + batch_product('bik,bjk->bij', grad_blocks, grad_blocks) / BLOCK
    right_gram = decay_rate * split_blocks(right_stats) + batch_product('bki,bkj->bij', grad_blocks, grad_blocks) / BLOCK
    block_total = grad_blocks.shape[0]
    roots = inverse_root(jnp.concatenate([left_gram, right_gram], 0))
    left_root = roots[:block_total]
    right_root = roots[block_total:]
    update = batch_product('bij,bjk->bik', batch_product('bij,bjk->bik', left_root, grad_blocks), right_root)
    update = join_blocks(update, D, F).astype(jnp.bfloat16)
    return (input_grad, update, join_blocks(left_gram, D, F), join_blocks(right_gram, D, F))
```

```python
import jax
import jax.numpy as jnp
from jax import lax
from jax.experimental import pallas as pl
from jax.experimental.pallas import tpu as pltpu
from jax.sharding import Mesh, PartitionSpec as P


BLOCK = 512
HALF = 256
ITERS = 10
DECAY = 0.9
F32 = jnp.float32
BF16 = jnp.bfloat16
AXES = ("x", "zh", "y", "zl", "c")
SIZES = (4, 2, 4, 2, 2)
VMEM_SPEC = pl.BlockSpec(memory_space=pltpu.VMEM)
SMEM_SPEC = pl.BlockSpec(memory_space=pltpu.SMEM)


def params(mib):
    return pltpu.CompilerParams(vmem_limit_bytes=mib << 20)


def linear(x, zh, y, zl, c):
    return (((x * 2 + zh) * 4 + y) * 2 + zl) * 2 + c


def exchange(value, target):
    pairs = []
    for x in range(4):
        for zh in range(2):
            for y in range(4):
                for zl in range(2):
                    for c in range(2):
                        to = target(x, zh, y, zl, c)
                        if to is not None:
                            pairs.append((linear(x, zh, y, zl, c), linear(*to)))
    return lax.ppermute(value, AXES, pairs)


def other_core(value):
    return exchange(value, lambda x, zh, y, zl, c: (x, zh, y, zl, 1 - c))


def across_y(value, mask):
    return exchange(value, lambda x, zh, y, zl, c: (x, zh, y ^ mask, zl, c))


def parts_of(value):
    high = value.astype(BF16)
    return high, (value - high.astype(F32)).astype(BF16)


def contract(first, second, dims):
    def one(a, b):
        return lax.dot_general(a, b, (dims, ((), ())), preferred_element_type=F32)

    return one(first[0], second[0]) + (one(first[0], second[1]) + one(first[1], second[0]))


def multiply(first, second):
    return contract(first, second, ((1,), (0,)))


def spread_kernel(flags, acts, grads, rows_out, cols_out):
    first = flags[0] == 0
    for i in range(2):
        start = i * BLOCK
        rows_out[0, :, i * HALF : (i + 1) * HALF] = jnp.where(
            first, acts[:, start : start + HALF], acts[:, start + HALF : start + BLOCK]
        )
    cols_out[0] = grads[...]


def spread(flags, acts, grads):
    shape = jax.ShapeDtypeStruct((8, 256, BLOCK), BF16)
    out_spec = pl.BlockSpec((1, 256, BLOCK), lambda i: (i, 0, 0))
    return pl.pallas_call(
        spread_kernel,
        grid=(8,),
        out_shape=[shape, shape],
        in_specs=[
            SMEM_SPEC,
            pl.BlockSpec((256, 1024), lambda i: (0, i)),
            pl.BlockSpec((256, BLOCK), lambda i: (0, 0)),
        ],
        out_specs=[out_spec, out_spec],
        compiler_params=params(56),
        cost_estimate=pl.CostEstimate(flops=0, bytes_accessed=8 << 20, transcendentals=0),
    )(flags, acts, grads)


def grad_kernel(flags, acts, own, other, *outs):
    core, y = flags[0], flags[1]
    same = (y % 2) == core
    upper = (y // 2) == 1
    for row in range(2):
        for take_own in (True, False):
            flip_high = jnp.where(upper, 1 - row, row)
            flip_low = jnp.where(same, 0 if take_own else 1, 1 if take_own else 0)
            value = lax.dot_general(
                acts[:, row * HALF : (row + 1) * HALF],
                (own if take_own else other)[...],
                (((0,), (0,)), ((), ())),
                preferred_element_type=F32,
            )
            for k in range(4):

                @pl.when(flip_high * 2 + flip_low == k)
                def _(k=k, value=value):
                    outs[k][...] = value


def grad_terms(flags, acts, own, other):
    return pl.pallas_call(
        grad_kernel,
        out_shape=[jax.ShapeDtypeStruct((HALF, BLOCK), F32)] * 4,
        in_specs=[SMEM_SPEC] + [VMEM_SPEC] * 3,
        out_specs=[VMEM_SPEC] * 4,
        compiler_params=params(24),
        cost_estimate=pl.CostEstimate(
            flops=2 * acts.shape[0] * BLOCK * 1024, bytes_accessed=8 << 20, transcendentals=0
        ),
    )(flags, acts, own, other)


def input_kernel(place, grads, weight, *rest):
    value = lax.dot_general(
        grads[...], weight[...], (((1,), (1,)), ((), ())), preferred_element_type=F32
    )
    if len(rest) == 2:
        value = value + rest[0][0]
        rest[1][...] = value
    else:
        rest[0][0] = value


def input_terms(place, grads, weight, added=None, which=None):
    tile = BLOCK
    pairs = 2 if which is None else 1
    base = 0 if which is None else which

    def rows(i, n, where):
        zl, core = where[0], where[1]
        zl = jnp.where(i + base == 0, zl, 1 - zl)
        return ((zl * 2 + core) * 4 + n, 0)

    in_specs = [
        pl.BlockSpec((256, BLOCK), lambda i, n, where: (0, 0)),
        pl.BlockSpec((tile, BLOCK), rows),
    ]
    operands = [grads, weight]
    if which is None:
        out_shape = jax.ShapeDtypeStruct((2, 256, 2048), F32)
        out_spec = pl.BlockSpec((1, 256, tile), lambda i, n, where: (i, 0, n))
    else:
        in_specs.append(pl.BlockSpec((1, 256, tile), lambda i, n, where: (which, 0, n)))
        operands.append(added)
        out_shape = jax.ShapeDtypeStruct((256, 2048), F32)
        out_spec = pl.BlockSpec((256, tile), lambda i, n, where: (0, n))
    return pl.pallas_call(
        input_kernel,
        out_shape=out_shape,
        grid_spec=pltpu.PrefetchScalarGridSpec(
            num_scalar_prefetch=1, grid=(pairs, 4), in_specs=in_specs, out_specs=out_spec
        ),
        compiler_params=params(56),
        cost_estimate=pl.CostEstimate(
            flops=pairs << 29, bytes_accessed=pairs << 22, transcendentals=0
        ),
    )(place, *operands)


def gram_kernel(flags, grad_own, grad_other, stat_self, stat_p1, stat_p2, stat_p3, grad, mine, opposite):
    core, low = flags[0], flags[1] % 2
    diagonal = core == low
    grad[pl.ds(pl.multiple_of(core * HALF, HALF), HALF), :] = grad_own[...]
    grad[pl.ds(pl.multiple_of((1 - core) * HALF, HALF), HALF), :] = grad_other[...]
    stat_mine = jnp.where(diagonal, stat_self[...], stat_p2[...])
    stat_opposite = jnp.where(diagonal, stat_p1[...], stat_p3[...])
    whole = parts_of(grad[...])

    def store(product):
        lower, upper = product[:HALF] * (1.0 / BLOCK), product[HALF:] * (1.0 / BLOCK)
        mine[...] = DECAY * stat_mine + jnp.where(low == 0, lower, upper)
        opposite[...] = DECAY * stat_opposite + jnp.where(low == 0, upper, lower)

    @pl.when(core == 0)
    def _():
        store(contract(whole, whole, ((1,), (1,))))

    @pl.when(core == 1)
    def _():
        store(contract(whole, whole, ((0,), (0,))))


def new_statistics(flags, grad_own, grad_other, stats):
    half = jax.ShapeDtypeStruct((HALF, BLOCK), F32)
    return pl.pallas_call(
        gram_kernel,
        out_shape=[jax.ShapeDtypeStruct((BLOCK, BLOCK), F32), half, half],
        in_specs=[SMEM_SPEC] + [VMEM_SPEC] * 6,
        out_specs=[VMEM_SPEC] * 3,
        compiler_params=params(20),
        cost_estimate=pl.CostEstimate(flops=6 * BLOCK**3, bytes_accessed=5 << 20, transcendentals=0),
    )(flags, grad_own, grad_other, *stats)


def quarters(values):
    s11, s12, s22 = (parts_of(v) for v in values)
    return s11, s12, parts_of(values[1].T), s22


def product(first, second):
    return (
        multiply(first[0], second[0]) + multiply(first[1], second[2]),
        multiply(first[0], second[1]) + multiply(first[1], second[3]),
        multiply(first[2], second[1]) + multiply(first[3], second[3]),
    )


def root_kernel(flags, mine, opposite, root, current, result):
    low = flags[1] % 2 == 0
    top = jnp.where(low, mine[...], opposite[...])
    bottom = jnp.where(low, opposite[...], mine[...])
    squares = top * top + bottom * bottom
    total = jnp.sum(jnp.sum(squares, axis=0, keepdims=True), axis=1, keepdims=True)
    frobenius = jnp.sqrt(total)
    inverse = 1.0 / frobenius
    rows = lax.broadcasted_iota(jnp.int32, (HALF, HALF), 0)
    unit = jnp.where(rows == lax.broadcasted_iota(jnp.int32, (HALF, HALF), 1), 1.25, 0.0)

    def load(ref):
        return [ref[0], ref[1], ref[2]]

    def store(ref, value):
        for j in range(3):
            ref[j] = value[j]

    def next_current(matrix, split):
        square = product(split, split)
        rest = quarters([square[j] * (1 / 16) - 0.625 * matrix[j] for j in range(3)])
        once = [1.5625 * matrix[j] + v for j, v in enumerate(product(rest, split))]
        twice = product(rest, quarters(once))
        store(current, [1.5625 * once[j] + twice[j] for j in range(3)])

    def next_result(split):
        value = load(result)
        moved = product(quarters(value), split)
        return [1.25 * value[j] - 0.25 * moved[j] for j in range(3)]

    store(current, [top[:, :HALF] * inverse, top[:, HALF:] * inverse, bottom[:, HALF:] * inverse])
    matrix = load(current)
    store(result, [unit - 0.25 * matrix[0], -0.25 * matrix[1], unit - 0.25 * matrix[2]])
    next_current(matrix, quarters(matrix))

    def step(_, carry):
        matrix = load(current)
        split = quarters(matrix)
        store(result, next_result(split))
        next_current(matrix, split)
        return carry

    lax.fori_loop(1, ITERS - 1, step, 0)
    value = next_result(quarters(load(current)))
    scale = 1.0 / jnp.sqrt(jnp.sqrt(frobenius))
    root[:HALF, :HALF] = value[0] * scale
    root[:HALF, HALF:] = value[1] * scale
    root[HALF:, :HALF] = value[1].T * scale
    root[HALF:, HALF:] = value[2] * scale


def inverse_root(flags, mine, opposite):
    return pl.pallas_call(
        root_kernel,
        out_shape=jax.ShapeDtypeStruct((BLOCK, BLOCK), F32),
        in_specs=[SMEM_SPEC] + [VMEM_SPEC] * 2,
        out_specs=VMEM_SPEC,
        scratch_shapes=[pltpu.VMEM((3, HALF, HALF), F32), pltpu.VMEM((3, HALF, HALF), F32)],
        compiler_params=params(20),
        cost_estimate=pl.CostEstimate(flops=200 * BLOCK**3, bytes_accessed=2 << 20, transcendentals=0),
    )(flags, mine, opposite)


def update_kernel(flags, own, peer, grad, out):
    core = flags[0]
    rows = pl.ds(pl.multiple_of(core * HALF, HALF), HALF)

    def store(left, right):
        first = multiply(parts_of(left), parts_of(grad[...]))
        out[...] = multiply(parts_of(first), parts_of(right)).astype(BF16)

    store(jnp.where(core == 0, own[rows, :], peer[rows, :]), jnp.where(core == 0, peer[...], own[...]))


def update_rows(flags, own, peer, grad):
    return pl.pallas_call(
        update_kernel,
        out_shape=jax.ShapeDtypeStruct((HALF, BLOCK), BF16),
        in_specs=[SMEM_SPEC] + [VMEM_SPEC] * 3,
        out_specs=VMEM_SPEC,
        compiler_params=params(20),
        cost_estimate=pl.CostEstimate(flops=6 * BLOCK**3, bytes_accessed=4 << 20, transcendentals=0),
    )(flags, own, peer, grad)


def body(activations, out_grad, weight, left_stats, right_stats):
    y, zl, core = lax.axis_index("y"), lax.axis_index("zl"), lax.axis_index("c")
    low = y % 2
    tokens = activations.shape[0] * 32
    flags = jnp.stack([core, y]).astype(jnp.int32)
    diagonal = core == low

    rows, cols = spread(flags, activations, out_grad)
    rows, cols, out_grad = lax.optimization_barrier((rows, cols, out_grad))
    own_cols = lax.all_to_all(cols, ("x", "zh"), 0, 0, tiled=True).reshape(-1, BLOCK)
    acts = lax.all_to_all(rows, ("x", "zh"), 0, 0, tiled=True).reshape(-1, BLOCK)
    other_cols = other_core(own_cols)

    own_kind = jnp.where(core == 0, left_stats, right_stats)
    other_kind = jnp.where(core == 0, right_stats, left_stats)
    stat_p1 = exchange(
        own_kind, lambda x, zh, y, zl, c: (x, zh, y ^ 1, zl, c) if y % 2 != c else None
    )
    stat_p2 = exchange(
        other_kind, lambda x, zh, y, zl, c: (x, zh, y, zl, 1 - c) if y % 2 == c else None
    )
    stat_p3 = exchange(
        other_kind, lambda x, zh, y, zl, c: (x, zh, y ^ 1, zl, 1 - c) if y % 2 != c else None
    )

    for_other = input_terms(jnp.stack([zl, 1 - core]).astype(jnp.int32), out_grad, weight)
    from_other = other_core(for_other)
    place = jnp.stack([zl, core]).astype(jnp.int32)
    sent = input_terms(place, out_grad, weight, from_other, 1)
    kept = input_terms(place, out_grad, weight, from_other, 0)

    acts, sent, kept, stat_p1, stat_p2, stat_p3 = lax.optimization_barrier(
        (acts, sent, kept, stat_p1, stat_p2, stat_p3)
    )
    came = exchange(sent, lambda x, zh, y, zl, c: (x, zh, y, 1 - zl, c))

    terms = grad_terms(flags, acts, own_cols, other_cols)
    arrived = [across_y(terms[k], k) for k in (1, 2, 3)]
    grad_half = (terms[0] + arrived[0] + arrived[1] + arrived[2]) * tokens ** (-0.5)
    grad, mine, opposite = new_statistics(
        flags, grad_half, other_core(grad_half), (own_kind, stat_p1, stat_p2, stat_p3)
    )
    out_p1 = exchange(
        opposite, lambda x, zh, y, zl, c: (x, zh, y ^ 1, zl, c) if y % 2 == c else None
    )
    out_p2 = exchange(mine, lambda x, zh, y, zl, c: (x, zh, y, zl, 1 - c) if y % 2 != c else None)
    out_p3 = exchange(
        opposite, lambda x, zh, y, zl, c: (x, zh, y ^ 1, zl, 1 - c) if y % 2 != c else None
    )
    root = inverse_root(flags, mine, opposite)
    update = update_rows(flags, root, other_core(root), grad)
    crossed = exchange(
        update, lambda x, zh, y, zl, c: (x, zh, y ^ 1, zl, 1 - c) if y % 2 != c else None
    )
    update = jnp.where(diagonal, update, crossed)
    left_rows = jnp.where(
        core == 0, jnp.where(low == 0, mine, out_p1), jnp.where(low == 0, out_p3, out_p2)
    )
    right_rows = jnp.where(
        core == 0, jnp.where(low == 0, out_p2, out_p3), jnp.where(low == 0, out_p1, mine)
    )
    input_grad = (kept + came).astype(BF16)
    return input_grad, update, left_rows, right_rows


def solution(mesh):
    wide = Mesh(mesh.devices.reshape(SIZES), AXES)
    dp, tensor = ("x", "zh", "y"), ("zl", "c")
    both = P(dp, tensor)
    return jax.shard_map(
        body,
        mesh=wide,
        in_specs=(P(dp, None), both, P(None, tensor), both, both),
        out_specs=(both, both, both, both),
        check_vma=False,
    )
```
